32 devices in a mesh: narrow: 4 (over y, x), wide: 8 (over z, core).
Axes of the slice: x: 2, y: 2, z: 4, core: 2. Of those that a mesh axis runs over, the one named last changes fastest.
Arguments:
- tokens: bfloat16 [32768, 768], P(('narrow', 'wide')), may hold values from -6 to 6
- frame_counts: int32 [32, 16], P(('narrow', 'wide')), may hold values from 8 to 32, as said below
- segment_ids: int32 [32768], P(('narrow', 'wide')), may hold values from 0 to 13, as said below
- positions: int32 [32768], P(('narrow', 'wide')), may hold values from 0 to 3135, as said below
- cotangent: bfloat16 [32768, 768], P(('narrow', 'wide')), may hold values from -6 to 6
- input_weight: bfloat16 [768, 2304], P('wide'), may hold values from -0.21875 to 0.21875
- output_weight: bfloat16 [768, 768], P('wide'), may hold values from -0.875 to 0.875
- up_weight: bfloat16 [768, 3072], P('wide'), may hold values from -0.21875 to 0.21875
- down_weight: bfloat16 [3072, 768], P('wide'), may hold values from -0.109375 to 0.109375
- pre_gain: bfloat16 [768], P('wide'), may hold values from 0.099609375 to 1.8984375
- pre_bias: bfloat16 [768], P('wide'), may hold values from -3 to 3
- query_bias: bfloat16 [768], P('wide'), may hold values from -3 to 3
- value_bias: bfloat16 [768], P('wide'), may hold values from -3 to 3
- output_bias: bfloat16 [768], P('wide'), may hold values from -3 to 3
- mid_gain: bfloat16 [768], P('wide'), may hold values from 0.099609375 to 1.8984375
- mid_bias: bfloat16 [768], P('wide'), may hold values from -3 to 3
- up_bias: bfloat16 [3072], P('wide'), may hold values from -3 to 3
- down_bias: bfloat16 [768], P('wide'), may hold values from -3 to 3
Outputs:
- block_out: bfloat16 [32768, 768], P(('narrow', 'wide'))
- input_grad: bfloat16 [32768, 768], P(('narrow', 'wide'))
- grad_input_weight: float32 [768, 2304], P('wide')
- grad_output_weight: float32 [768, 768], P('wide')
- grad_up_weight: float32 [768, 3072], P('wide')
- grad_down_weight: float32 [3072, 768], P('wide')
- grad_pre_gain: float32 [768], P('wide')
- grad_pre_bias: float32 [768], P('wide')
- grad_query_bias: float32 [768], P('wide')
- grad_value_bias: float32 [768], P('wide')
- grad_output_bias: float32 [768], P('wide')
- grad_mid_gain: float32 [768], P('wide')
- grad_mid_bias: float32 [768], P('wide')
- grad_up_bias: float32 [3072], P('wide')
- grad_down_bias: float32 [768], P('wide')
The draws below stay inside these ranges and needn't reach their ends.
Inputs may be any that keep to these rules, and one draw needn't show every extreme that they name: `frame_counts`: each packed sequence fills its clip slots in order; a slot's clip has 8, 16 or 32 frames, short clips being the most common; slots that the sequence's rows never reach still hold a frame count. `segment_ids`: within a sequence the slot number never falls and starts at 0; a clip of 8, 16 or 32 frames holds 78, 157 or 314 rows times 1024 / 1024 (rounded down, at least 1), except that the sequence's end may cut its last clip. `positions`: index of a row's tubelet in its clip's grid of (frames / 2) x 14 x 14 tubelets, below that grid's size.
All inputs are finite; a program needn't handle non-finite values.
Results may differ from the reference program's by a relative error of at most 0.019.
Values may be sent and summed in bfloat16 or wider, within the bound.
No kernel may reach another device: no remote copies, remote signals or barrier semaphores. Data moves between devices by JAX's collectives and lax.ppermute only.
A program may use at most 192 MiB of HBM per device.

```python
import math
import jax
import jax.numpy as jnp
from jax import lax

D = 768
HEADS = 12
HEAD_DIM = 64
FF = 3072
SEQ = 1024
CLIPS = 16
SEQS = 32
TOKENS = 32768


def packing(key):
    kind_key = jax.random.fold_in(key, 11)
    jitter_key = jax.random.fold_in(key, 23)
    dice = jax.random.randint(kind_key, (SEQS, CLIPS), 0, 8)
    kind = jnp.where(dice < 5, 0, jnp.where(dice < 7, 1, 2)).astype(jnp.int32)
    kind = kind.at[SEQS - 1, :].set(0)
    kind = kind.at[0, 0].set(2).at[0, 1].set(0)
    base = jnp.where(kind == 0, 78, jnp.where(kind == 1, 157, 314)).astype(jnp.int32)
    clip_length = jnp.maximum(1, base * SEQ // 1024)
    ends = jnp.cumsum(clip_length, axis=1)
    starts = ends - clip_length
    row_index = jnp.arange(SEQ, dtype=jnp.int32)
    labels = jnp.sum((ends[:, :, None] <= row_index[None, None, :]).astype(jnp.int32), axis=1)
    start_row = jnp.take_along_axis(starts, labels, axis=1)
    length_row = jnp.take_along_axis(clip_length, labels, axis=1)
    offset = row_index[None, :] - start_row
    frames = jnp.where(kind == 0, 8, jnp.where(kind == 1, 16, 32)).astype(jnp.int32)
    grid = frames // 2 * 196
    grid_row = jnp.take_along_axis(grid, labels, axis=1)
    jitter = jax.random.randint(jitter_key, (SEQS, SEQ), 0, 10)
    spaced = jnp.minimum(offset * 10 + jitter, grid_row - 1)
    position_ids = jnp.where(offset == length_row - 1, grid_row - 1, spaced)
    return (frames, labels.reshape(-1).astype(jnp.int32), position_ids.reshape(-1).astype(jnp.int32))


def draw_frame_counts(key, part):
    return packing(key)[0]


def draw_segment_ids(key, part):
    return packing(key)[1]


def draw_positions(key, part):
    return packing(key)[2]


def levels(stream_key, extent, shards, least, largest):
    factor_of = 1.0
    for position, parts in shards:
        steps = jax.random.uniform(jax.random.fold_in(jax.random.fold_in(stream_key, 6), position), (parts,), jnp.float32, least / len(shards), largest / len(shards))
        factor_of = factor_of * jnp.repeat(jnp.exp(steps), extent[position] // parts).reshape((-1,) + (1,) * (len(extent) - 1 - position))
    return factor_of


def normal_values(key, extent, scale, bound, cuts=(), kind=jnp.bfloat16):
    array = scale * jax.random.normal(key, extent, jnp.float32)
    if cuts:
        array = array * levels(key, extent, cuts, -0.22, 0.18)
    return jnp.clip(array, -bound, bound).astype(kind)


def setup_inputs(seed: int = 0) -> dict:
    seeds = jax.random.split(jax.random.key(seed), 19)
    return {
        "tokens": normal_values(seeds[0], (TOKENS, D), 1.0, 6.0, ((0, 32),)),
        "frame_counts": draw_frame_counts(jax.random.fold_in(seeds[18], 71), 0),
        "segment_ids": draw_segment_ids(jax.random.fold_in(seeds[18], 71), 0),
        "positions": draw_positions(jax.random.fold_in(seeds[18], 71), 0),
        "cotangent": normal_values(seeds[4], (TOKENS, D), 1.0, 6.0, ((0, 32),)),
        "input_weight": normal_values(seeds[5], (D, 3 * D), D ** -0.5, 0.21875, ((0, 8),)),
        "output_weight": normal_values(seeds[6], (D, D), (D // 16) ** -0.5, 0.875, ((0, 8),)),
        "up_weight": normal_values(seeds[7], (D, FF), D ** -0.5, 0.21875, ((0, 8),)),
        "down_weight": normal_values(seeds[8], (FF, D), FF ** -0.5, 0.109375, ((0, 8),)),
        "pre_gain": jnp.clip(1.0 + 0.18 * jax.random.normal(seeds[9], (D,), jnp.float32), 0.099609375, 1.8984375).astype(jnp.bfloat16),
        "pre_bias": normal_values(seeds[10], (D,), 0.5, 3.0, ((0, 8),)),
        "query_bias": normal_values(seeds[11], (D,), 0.5, 3.0, ((0, 8),)),
        "value_bias": normal_values(seeds[12], (D,), 0.5, 3.0, ((0, 8),)),
        "output_bias": normal_values(seeds[13], (D,), 0.5, 3.0, ((0, 8),)),
        "mid_gain": jnp.clip(1.0 + 0.18 * jax.random.normal(seeds[14], (D,), jnp.float32), 0.099609375, 1.8984375).astype(jnp.bfloat16),
        "mid_bias": normal_values(seeds[15], (D,), 0.5, 3.0, ((0, 8),)),
        "up_bias": normal_values(seeds[16], (FF,), 0.5, 3.0, ((0, 8),)),
        "down_bias": normal_values(seeds[17], (D,), 0.5, 3.0, ((0, 8),)),
    }


highest = lax.Precision.HIGHEST

@jax.custom_vjp
def low(v):
    return lax.optimization_barrier(v.astype(jnp.bfloat16)).astype(jnp.float32)

@jax.custom_vjp
def low_back(v):
    return v

def low_keep(v):
    return (low(v), None)

def low_pass(kept, grad):
    return (grad,)

def back_keep(v):
    return (v, None)

def back_low(kept, grad):
    return (low(grad),)
low.defvjp(low_keep, low_pass)
low_back.defvjp(back_keep, back_low)

def layer_norm(values, gain, shift):
    center = values - lax.optimization_barrier(jnp.mean(values, axis=-1, keepdims=True))
    spread = lax.optimization_barrier(jnp.mean(center * center, axis=-1, keepdims=True))
    return center * lax.rsqrt(spread + 1e-06) * gain + shift

def position_table(position_ids, frame_row):
    tubelet = position_ids // 196
    within = position_ids % 196
    first = tubelet.astype(jnp.float32) * 16.0 / frame_row.astype(jnp.float32)
    second = (within // 14).astype(jnp.float32)
    third = (within % 14).astype(jnp.float32)
    channel = jnp.arange(D, dtype=jnp.int32)
    picker = (channel % 3)[None, :]
    rate = jnp.exp(-(6.0 * (channel // 6).astype(jnp.float32) / D) * math.log(10000.0))
    coordinate = jnp.where(picker == 0, first[:, None], jnp.where(picker == 1, second[:, None], third[:, None]))
    angle = coordinate * rate[None, :]
    return jnp.where((channel // 3 % 2)[None, :] == 1, jnp.cos(angle), jnp.sin(angle))

def attend_one(packed):
    queries, key_rows, values, labels = packed
    raw_scores = jnp.einsum('qhd,khd->hqk', queries, key_rows, precision=highest)
    scores = low_back(raw_scores) * HEAD_DIM ** (-0.5)
    allowed = labels[:, None] == labels[None, :]
    scores = jnp.where(allowed[None], scores, -1e+30)
    peak_score = lax.optimization_barrier(jnp.max(scores, axis=-1, keepdims=True))
    expo_scores = jnp.exp(scores - peak_score)
    probabilities = expo_scores / lax.optimization_barrier(jnp.sum(expo_scores, axis=-1, keepdims=True))
    return jnp.einsum('hqk,khd->qhd', low(probabilities), values, precision=highest)

def block_forward(start, weights, labels):
    input_weight, output_weight, up_weight, down_weight, pre_gain, pre_bias, query_bias, value_bias, output_bias, mid_gain, mid_bias, up_bias, down_bias = weights
    row_total = start.shape[0]
    seq_count = row_total // SEQ
    normed = low(layer_norm(start, pre_gain, pre_bias))
    joint_bias = jnp.concatenate([query_bias, jnp.zeros_like(query_bias), value_bias])
    mixed = jnp.dot(normed, input_weight, precision=highest) + joint_bias
    mixed = low(low_back(mixed))
    split = mixed.reshape(seq_count, SEQ, 3, HEADS, HEAD_DIM)
    attended = lax.map(jax.checkpoint(attend_one), (split[:, :, 0], split[:, :, 1], split[:, :, 2], labels))
    attended = low(low_back(attended.reshape(row_total, D)))
    branch = low_back(jnp.dot(attended, output_weight, precision=highest) + output_bias)
    middle = start + branch
    normed_two = low(layer_norm(middle, mid_gain, mid_bias))
    upward = low_back(jnp.dot(normed_two, up_weight, precision=highest) + up_bias)
    active = low(jax.nn.gelu(upward, approximate=False))
    return middle + low_back(jnp.dot(active, down_weight, precision=highest) + down_bias)

def reference(tokens, frame_counts, segment_ids, positions, cotangent, input_weight, output_weight, up_weight, down_weight, pre_gain, pre_bias, query_bias, value_bias, output_bias, mid_gain, mid_bias, up_bias, down_bias):
    row_total = tokens.shape[0]
    seq_count = row_total // SEQ
    group = math.gcd(seq_count, max(1, 4096 // SEQ))
    group_count = seq_count // group
    seq_of_row = jnp.arange(row_total, dtype=jnp.int32) // SEQ
    frame_row = frame_counts[seq_of_row, segment_ids]
    table = position_table(positions, frame_row)
    params = tuple((member.astype(jnp.float32) for member in (input_weight, output_weight, up_weight, down_weight, pre_gain, pre_bias, query_bias, value_bias, output_bias, mid_gain, mid_bias, up_bias, down_bias)))

    def one_group(totals, packed):
        rows_in, table_in, labels, back_in = packed

        def forward_fn(begin, weights):
            return block_forward(begin + table_in, weights, labels.reshape(group, SEQ))
        result, pullback = jax.vjp(forward_fn, rows_in, params)
        grad_rows, grad_params = pullback(back_in)
        totals = jax.tree.map(jnp.add, totals, grad_params)
        return (totals, (result, grad_rows))
    zeros = jax.tree.map(jnp.zeros_like, params)
    packed = (tokens.astype(jnp.float32).reshape(group_count, group * SEQ, D), table.reshape(group_count, group * SEQ, D), segment_ids.reshape(group_count, group * SEQ), cotangent.astype(jnp.float32).reshape(group_count, group * SEQ, D))
    totals, (results, grads) = lax.scan(one_group, zeros, packed)
    return (results.reshape(row_total, D).astype(jnp.bfloat16), grads.reshape(row_total, D).astype(jnp.bfloat16), totals[0], totals[1], totals[2], totals[3], totals[4], totals[5], totals[6], totals[7], totals[8], totals[9], totals[10], totals[11], totals[12])
```

```python
from functools import partial
import math

import jax
import jax.numpy as jnp
from jax import lax
from jax.experimental import pallas as pl
from jax.experimental.pallas import tpu as pltpu
from jax.sharding import PartitionSpec as P

D = 768
HEADS = 12
HEAD_DIM = 64
LANES = 128
TILE = 128
PARTS = 3
FF_BLOCK = 512
SQRT_HALF = math.sqrt(0.5)
INV_SQRT_2PI = 1.0 / math.sqrt(2.0 * math.pi)
VMEM_BYTES = 60000 * 1024


def dot(a, b, ca, cb):
    return lax.dot_general(a, b, (((ca,), (cb,)), ((), ())), preferred_element_type=jnp.float32)


def widths_for(length):
    return [w for w in (256, 384, 512, 768) if w < length] + [length]


def select_width(length, tile, low, high, run):
    first = low[tile]
    count = high[tile] - first
    previous = 0
    for width in widths_for(length):
        tiles = width // TILE

        @pl.when(jnp.logical_and(count > previous, count <= tiles))
        def _(width=width, tiles=tiles):
            start = jnp.minimum(first, length // TILE - tiles) * TILE
            run(width, pl.multiple_of(start, TILE))

        previous = tiles


def stack_heads(pair, lane_low):
    zero = jnp.zeros_like(pair)
    return jnp.concatenate([jnp.where(lane_low, pair, zero), jnp.where(lane_low, zero, pair)], axis=0)


def attend_kernel(low, high, mixed, label_col, label_row, attended, log_mass):
    length = mixed.shape[0]
    tile = pl.program_id(0)
    rows = pl.ds(pl.multiple_of(tile * TILE, TILE), TILE)
    lane = lax.broadcasted_iota(jnp.int32, (TILE, LANES), 1)
    lane_low = lane < HEAD_DIM

    def run(width, start):
        keys = pl.ds(start, width)
        allowed = label_col[rows, :] == label_row[:, keys]
        bias = jnp.where(allowed, 0.0, -1e30)
        bias = jnp.concatenate([bias, bias], axis=0)

        def pair_step(pair, masses):
            offset = pl.multiple_of(pair * LANES, LANES)
            query = mixed[rows, pl.ds(offset, LANES)] * jnp.bfloat16(0.125)
            key = mixed[keys, pl.ds(offset + D, LANES)]
            value = mixed[keys, pl.ds(offset + 2 * D, LANES)]
            scores = dot(stack_heads(query, lane_low), key, 1, 1) + bias
            peak = jnp.max(scores, axis=1, keepdims=True)
            expo = jnp.exp(scores - peak)
            total = jnp.sum(expo, axis=1, keepdims=True)
            both = dot(expo.astype(jnp.bfloat16), value, 1, 0) / total
            attended[:, pl.ds(offset, LANES)] = jnp.where(
                lane_low, both[:TILE], both[TILE:]
            ).astype(jnp.bfloat16)
            mass = peak + jnp.log(total)
            masses = jnp.where(lane == 2 * pair, mass[:TILE], masses)
            return jnp.where(lane == 2 * pair + 1, mass[TILE:], masses)

        log_mass[...] = lax.fori_loop(
            0, HEADS // 2, pair_step, jnp.zeros((TILE, LANES), jnp.float32)
        )

    select_width(length, tile, low, high, run)


def attend_back_kernel(
    low, high, mixed, label_col, label_row, log_mass, attended, grad_att, grad_mixed, key_acc, value_acc
):
    length = mixed.shape[0]
    tile = pl.program_id(0)
    rows = pl.ds(pl.multiple_of(tile * TILE, TILE), TILE)
    lane = lax.broadcasted_iota(jnp.int32, (TILE, LANES), 1)
    lane_low = lane < HEAD_DIM

    @pl.when(tile == 0)
    def _():
        key_acc[...] = jnp.zeros_like(key_acc)
        value_acc[...] = jnp.zeros_like(value_acc)

    def run(width, start):
        keys = pl.ds(start, width)
        allowed = label_col[rows, :] == label_row[:, keys]
        bias = jnp.where(allowed, 0.0, -1e30)
        bias = jnp.concatenate([bias, bias], axis=0)
        masses = log_mass[...]

        def pair_step(pair, carry):
            offset = pl.multiple_of(pair * LANES, LANES)
            lanes = pl.ds(offset, LANES)
            query = stack_heads(mixed[rows, lanes] * jnp.bfloat16(0.125), lane_low)
            key = mixed[keys, pl.ds(offset + D, LANES)]
            value = mixed[keys, pl.ds(offset + 2 * D, LANES)]
            grad = grad_att[:, lanes]
            product = grad.astype(jnp.float32) * attended[:, lanes].astype(jnp.float32)
            delta = jnp.concatenate(
                [
                    jnp.sum(jnp.where(lane_low, product, 0.0), axis=1, keepdims=True),
                    jnp.sum(jnp.where(lane_low, 0.0, product), axis=1, keepdims=True),
                ],
                axis=0,
            )
            mass = jnp.concatenate(
                [
                    jnp.sum(jnp.where(lane == 2 * pair, masses, 0.0), axis=1, keepdims=True),
                    jnp.sum(jnp.where(lane == 2 * pair + 1, masses, 0.0), axis=1, keepdims=True),
                ],
                axis=0,
            )
            grad_two = stack_heads(grad, lane_low)
            probs = jnp.exp(dot(query, key, 1, 1) + bias - mass)
            grad_probs = dot(grad_two, value, 1, 1)
            grad_scores = (probs * (grad_probs - delta)).astype(jnp.bfloat16)
            grad_query = dot(grad_scores, key, 1, 0) * 0.125
            grad_mixed[rows, lanes] = jnp.where(
                lane_low, grad_query[:TILE], grad_query[TILE:]
            ).astype(jnp.bfloat16)
            key_acc[keys, lanes] += dot(grad_scores, query, 0, 0)
            value_acc[keys, lanes] += dot(probs.astype(jnp.bfloat16), grad_two, 0, 0)
            return carry

        lax.fori_loop(0, HEADS // 2, pair_step, 0)

    select_width(length, tile, low, high, run)

    @pl.when(tile == pl.num_programs(0) - 1)
    def _():
        grad_mixed[:, D : 2 * D] = key_acc[...].astype(jnp.bfloat16)
        grad_mixed[:, 2 * D :] = value_acc[...].astype(jnp.bfloat16)


def attention_specs(length):
    whole = lambda i, *_: (0, 0)
    tiled = lambda i, *_: (i, 0)
    once = pl.Buffered(1)
    return (
        pl.BlockSpec((length, 3 * D), whole, pipeline_mode=once),
        pl.BlockSpec((length, 1), whole, pipeline_mode=once),
        pl.BlockSpec((1, length), whole, pipeline_mode=once),
        pl.BlockSpec((TILE, LANES), tiled),
        pl.BlockSpec((TILE, D), tiled),
    )


def attend(mixed, labels, low, high):
    length = mixed.shape[0]
    mixed_spec, col_spec, row_spec, mass_spec, rows_spec = attention_specs(length)
    return pl.pallas_call(
        attend_kernel,
        grid_spec=pltpu.PrefetchScalarGridSpec(
            num_scalar_prefetch=2,
            grid=(length // TILE,),
            in_specs=[mixed_spec, col_spec, row_spec],
            out_specs=[rows_spec, mass_spec],
        ),
        out_shape=[
            jax.ShapeDtypeStruct((length, D), jnp.bfloat16),
            jax.ShapeDtypeStruct((length, LANES), jnp.float32),
        ],
        compiler_params=pltpu.CompilerParams(vmem_limit_bytes=VMEM_BYTES),
        cost_estimate=pl.CostEstimate(
            flops=4 * length * 512 * D, bytes_accessed=length * 5 * D * 2, transcendentals=length * 512 * HEADS
        ),
        name="attend",
    )(low, high, mixed, labels[:, None], labels[None, :])


def attend_back(mixed, labels, low, high, log_mass, attended, grad_att):
    length = mixed.shape[0]
    mixed_spec, col_spec, row_spec, mass_spec, rows_spec = attention_specs(length)
    return pl.pallas_call(
        attend_back_kernel,
        grid_spec=pltpu.PrefetchScalarGridSpec(
            num_scalar_prefetch=2,
            grid=(length // TILE,),
            in_specs=[mixed_spec, col_spec, row_spec, mass_spec, rows_spec, rows_spec],
            out_specs=pl.BlockSpec((length, 3 * D), lambda i, *_: (0, 0)),
            scratch_shapes=[pltpu.VMEM((length, D), jnp.float32)] * 2,
        ),
        out_shape=jax.ShapeDtypeStruct((length, 3 * D), jnp.bfloat16),
        compiler_params=pltpu.CompilerParams(vmem_limit_bytes=VMEM_BYTES),
        cost_estimate=pl.CostEstimate(
            flops=10 * length * 512 * D, bytes_accessed=length * 9 * D * 2, transcendentals=length * 512 * HEADS
        ),
        name="attend_back",
    )(low, high, mixed, labels[:, None], labels[None, :], log_mass, attended, grad_att)


def feed_kernel(
    normed, cotangent, up, down, up_bias, out_in, back_in,
    out, back, grad_up, grad_down, grad_bias, active_all, grad_all,
):
    step = pl.program_id(0)
    length = normed.shape[0]
    chunk = 256

    @pl.when(step == 0)
    def _():
        grad_bias[...] = jnp.zeros_like(grad_bias)

    def row_step(index, total):
        rows = pl.ds(pl.multiple_of(index * chunk, chunk), chunk)
        upward = dot(normed[rows, :], up[...], 1, 0) + up_bias[...]
        normal = 0.5 * (1.0 + lax.erf(upward * SQRT_HALF))
        density = jnp.exp(-0.5 * upward * upward) * INV_SQRT_2PI
        active = (upward * normal).astype(jnp.bfloat16)
        active_all[rows, :] = active
        grad_active = dot(cotangent[rows, :], down[...], 1, 1)
        grad_up_f = grad_active * (normal + upward * density)
        grad_low = grad_up_f.astype(jnp.bfloat16)
        grad_all[rows, :] = grad_low
        forward = dot(active, down[...], 1, 0)
        backward = dot(grad_low, up[...], 1, 1)

        @pl.when(step == 0)
        def _():
            out[rows, :] = out_in[rows, :] + forward
            back[rows, :] = back_in[rows, :] + backward

        @pl.when(step > 0)
        def _():
            out[rows, :] += forward
            back[rows, :] += backward

        return total + jnp.sum(grad_low.astype(jnp.float32), axis=0, keepdims=True)

    total = lax.fori_loop(
        0, length // chunk, row_step, jnp.zeros((1, up.shape[1]), jnp.float32)
    )
    grad_bias[...] = total
    grad_up[...] = dot(normed[...], grad_all[...], 0, 0).astype(jnp.bfloat16)
    grad_down[...] = dot(active_all[...], cotangent[...], 0, 0).astype(jnp.bfloat16)


def feed_part(normed, cotangent, up, down, up_bias, out_in, back_in):
    length = normed.shape[0]
    hidden = up.shape[1]
    block = min(FF_BLOCK, hidden)
    steps = hidden // block
    whole = lambda i: (0, 0)
    once = pl.Buffered(1)
    full = lambda: pl.BlockSpec((length, D), whole, pipeline_mode=once)
    return pl.pallas_call(
        feed_kernel,
        grid=(steps,),
        in_specs=[
            full(),
            full(),
            pl.BlockSpec((D, block), lambda i: (0, i)),
            pl.BlockSpec((block, D), lambda i: (i, 0)),
            pl.BlockSpec((1, block), lambda i: (0, i)),
            full(),
            full(),
        ],
        out_specs=[
            pl.BlockSpec((length, D), whole),
            pl.BlockSpec((length, D), whole),
            pl.BlockSpec((D, block), lambda i: (0, i)),
            pl.BlockSpec((block, D), lambda i: (i, 0)),
            pl.BlockSpec((1, block), lambda i: (0, i)),
        ],
        out_shape=[
            jax.ShapeDtypeStruct((length, D), jnp.float32),
            jax.ShapeDtypeStruct((length, D), jnp.float32),
            jax.ShapeDtypeStruct((D, hidden), jnp.bfloat16),
            jax.ShapeDtypeStruct((hidden, D), jnp.bfloat16),
            jax.ShapeDtypeStruct((1, hidden), jnp.float32),
        ],
        scratch_shapes=[pltpu.VMEM((length, block), jnp.bfloat16)] * 2,
        compiler_params=pltpu.CompilerParams(vmem_limit_bytes=VMEM_BYTES),
        cost_estimate=pl.CostEstimate(
            flops=12 * length * hidden * D,
            bytes_accessed=length * D * 20 + hidden * D * 8,
            transcendentals=2 * length * hidden,
        ),
        name="feed_part",
    )(normed, cotangent, up, down, up_bias, out_in, back_in)


def position_rows(position_ids, frame_row):
    tubelet = position_ids // 196
    within = position_ids % 196
    halves = tubelet * 32 // frame_row
    channel = jnp.arange(D, dtype=jnp.int32)
    rate = jnp.exp(-(6.0 * (channel // 6).astype(jnp.float32) / D) * math.log(10000.0))
    entry = jnp.arange(48, dtype=jnp.int32)
    which = entry // 16
    level = (entry % 16).astype(jnp.float32) * jnp.where(which == 0, 0.5, 1.0)
    angle = level[:, None] * rate[None, :]
    values = jnp.where((channel // 3 % 2)[None, :] == 1, jnp.cos(angle), jnp.sin(angle))
    values = jnp.where(which[:, None] == (channel % 3)[None, :], values, 0.0)
    first = lax.reduce_precision(values, 8, 7)
    second = lax.reduce_precision(values - first, 8, 7)
    third = values - first - second
    table = jnp.concatenate([first, second, third], axis=0).astype(jnp.bfloat16)
    picks = [
        (index[:, None] + 16 * number) == entry[None, :]
        for number, index in enumerate((halves, within // 14, within % 14))
    ]
    hot = (picks[0] | picks[1] | picks[2]).astype(jnp.bfloat16)
    hot = jnp.concatenate([hot, hot, hot], axis=1)
    return jnp.dot(hot, table, preferred_element_type=jnp.float32)


def norm_parts(values):
    center = values - jnp.mean(values, axis=-1, keepdims=True)
    spread = jnp.mean(center * center, axis=-1, keepdims=True)
    rstd = lax.rsqrt(spread + 1e-06)
    return center * rstd, rstd


def norm_back(hat, rstd, gain, grad):
    e = grad * gain
    return rstd * (
        e - jnp.mean(e, axis=-1, keepdims=True) - hat * jnp.mean(e * hat, axis=-1, keepdims=True)
    )


def gather(values):
    return lax.all_gather(values, "wide", axis=0, tiled=True)


def scatter(values):
    return lax.psum_scatter(values, "wide", scatter_dimension=0, tiled=True)


def per_device(narrow, wide, *args):
    (
        tokens, frame_counts, segment_ids, positions, cotangent,
        input_weight, output_weight, up_weight, down_weight,
        pre_gain, pre_bias, query_bias, value_bias, output_bias,
        mid_gain, mid_bias, up_bias, down_bias,
    ) = args
    length = tokens.shape[0]
    rows = pre_gain.shape[0]
    sub = down_weight.shape[0] // PARTS

    def sum_copies(values):
        half = values.shape[0] // 2
        pieces = [values[:half], values[half:]]
        bits = [1 << k for k in range(narrow.bit_length() - 1)]
        outs = []
        for piece, order in zip(pieces, (bits, bits[::-1])):
            for bit in order:
                other = lax.ppermute(piece, "narrow", [(i, i ^ bit) for i in range(narrow)])
                piece = (piece.astype(jnp.float32) + other.astype(jnp.float32)).astype(jnp.bfloat16)
            outs.append(piece)
        return jnp.concatenate(outs, axis=0)

    quarters = up_bias.shape[0] // rows
    vectors = jnp.concatenate(
        [pre_gain, pre_bias, query_bias, value_bias, output_bias, mid_gain, mid_bias, down_bias, up_bias]
    ).reshape(8 + quarters, rows)
    vectors = jnp.pad(vectors, ((0, LANES - 8 - quarters), (0, 0))).T
    full_input = gather(jnp.concatenate([input_weight, vectors], axis=1))
    full_vectors = full_input[:, 3 * D :].T.astype(jnp.float32)
    full_input = full_input[:, : 3 * D]
    full_output = gather(output_weight)
    g_pre, b_pre, b_query, b_value, b_output, g_mid, b_mid, b_down = [full_vectors[k] for k in range(8)]
    full_up_bias = full_vectors[8 : 8 + quarters].reshape(quarters, wide, rows)
    full_up_bias = full_up_bias.transpose(1, 0, 2).reshape(wide, PARTS, sub)
    up_parts = up_weight.reshape(rows, wide, PARTS, sub)
    full_up = [gather(up_parts[:, :, k].reshape(rows, wide * sub)) for k in range(PARTS)]
    full_down = [gather(down_weight[k * sub : (k + 1) * sub]) for k in range(PARTS)]

    clip_index = jnp.arange(frame_counts.shape[1], dtype=jnp.int32)
    frame_row = jnp.sum(
        jnp.where(segment_ids[:, None] == clip_index[None, :], frame_counts, 0), axis=1
    )
    start = tokens.astype(jnp.float32) + position_rows(positions, frame_row)
    start = lax.optimization_barrier(start)
    hat, rstd = norm_parts(start)
    normed = (hat * g_pre + b_pre).astype(jnp.bfloat16)
    joint_bias = jnp.concatenate([b_query, jnp.zeros_like(b_query), b_value])
    mixed = (jnp.dot(normed, full_input, preferred_element_type=jnp.float32) + joint_bias).astype(
        jnp.bfloat16
    )
    tiles = segment_ids.reshape(length // TILE, TILE)
    low = jnp.sum((segment_ids[None, :] < tiles[:, :1]).astype(jnp.int32), axis=1) // TILE
    high = (
        jnp.sum((segment_ids[None, :] <= tiles[:, -1:]).astype(jnp.int32), axis=1) + TILE - 1
    ) // TILE
    attended, log_mass = attend(mixed, segment_ids, low, high)
    middle = (
        start + jnp.dot(attended, full_output, preferred_element_type=jnp.float32) + b_output
    )
    middle = lax.optimization_barrier(middle)
    hat_two, rstd_two = norm_parts(middle)
    normed_two = (hat_two * g_mid + b_mid).astype(jnp.bfloat16)

    out_sum = middle + b_down
    back_sum = jnp.zeros_like(middle)
    up_shares, down_shares, bias_parts = [], [], []
    for k in range(PARTS):
        out_sum, back_sum, grad_up, grad_down, grad_bias = feed_part(
            normed_two, cotangent, full_up[k], full_down[k],
            full_up_bias[:, k].reshape(1, wide * sub), out_sum, back_sum,
        )
        up_shares.append(sum_copies(scatter(grad_up)))
        down_shares.append(sum_copies(scatter(grad_down)))
        bias_parts.append(grad_bias.reshape(wide, sub))
    block_out = out_sum.astype(jnp.bfloat16)
    grad_top = cotangent.astype(jnp.float32)
    grad_middle = grad_top + norm_back(hat_two, rstd_two, g_mid, back_sum)
    grad_middle = lax.optimization_barrier(grad_middle)
    branch = grad_middle.astype(jnp.bfloat16)
    grad_up_bias = jnp.stack(bias_parts, axis=1).reshape(wide, quarters, rows)
    grad_up_bias = grad_up_bias.transpose(1, 0, 2).reshape(quarters, D)
    first_vectors = jnp.concatenate(
        [
            jnp.stack(
                [
                    jnp.sum(branch.astype(jnp.float32), axis=0),
                    jnp.sum(back_sum * hat_two, axis=0),
                    jnp.sum(back_sum, axis=0),
                    jnp.sum(grad_top, axis=0),
                ]
            ),
            grad_up_bias,
            jnp.zeros((LANES - 4 - quarters, D), jnp.float32),
        ]
    ).astype(jnp.bfloat16)
    grad_output = dot(attended, branch, 0, 0).astype(jnp.bfloat16)
    output_share = sum_copies(scatter(jnp.concatenate([grad_output, first_vectors.T], axis=1)))

    grad_att = dot(branch, full_output, 1, 1).astype(jnp.bfloat16)
    grad_mixed = attend_back(mixed, segment_ids, low, high, log_mass, attended, grad_att)
    grad_input = dot(normed, grad_mixed, 0, 0).astype(jnp.bfloat16)
    grad_normed = dot(grad_mixed, full_input, 1, 1)
    grad_normed = lax.optimization_barrier(grad_normed)
    mixed_sum = jnp.sum(grad_mixed.astype(jnp.float32), axis=0)
    last_vectors = jnp.concatenate(
        [
            jnp.stack(
                [
                    jnp.sum(grad_normed * hat, axis=0),
                    jnp.sum(grad_normed, axis=0),
                    mixed_sum[:D],
                    mixed_sum[2 * D :],
                ]
            ),
            jnp.zeros((LANES - 4, D), jnp.float32),
        ]
    ).astype(jnp.bfloat16)
    input_share = sum_copies(scatter(jnp.concatenate([grad_input, last_vectors.T], axis=1)))
    input_grad = (grad_middle + norm_back(hat, rstd, g_pre, grad_normed)).astype(jnp.bfloat16)

    f32 = lambda values: values.astype(jnp.float32)
    out_up = jnp.stack([s.reshape(rows, wide, sub) for s in up_shares], axis=2)
    first_rows = f32(output_share[:, D:]).T
    last_rows = f32(input_share[:, 3 * D :]).T
    return (
        block_out,
        input_grad,
        f32(input_share[:, : 3 * D]),
        f32(output_share[:, :D]),
        f32(out_up.reshape(rows, -1)),
        f32(jnp.concatenate(down_shares, axis=0)),
        last_rows[0],
        last_rows[1],
        last_rows[2],
        last_rows[3],
        first_rows[0],
        first_rows[1],
        first_rows[2],
        first_rows[4 : 4 + quarters].reshape(-1),
        first_rows[3],
    )


def solution(mesh):
    both = ("narrow", "wide")
    in_specs = (
        (P(both, None), P(both, None), P(both), P(both), P(both, None))
        + (P("wide", None),) * 4
        + (P("wide"),) * 9
    )
    out_specs = (P(both, None),) * 2 + (P("wide", None),) * 4 + (P("wide"),) * 9
    return jax.shard_map(
        partial(per_device, mesh.shape["narrow"], mesh.shape["wide"]),
        mesh=mesh, in_specs=in_specs, out_specs=out_specs, check_vma=False,
    )
```

```python
from functools import partial
import math

import jax
import jax.numpy as jnp
from jax import lax
from jax.experimental import pallas as pl
from jax.experimental.pallas import tpu as pltpu
from jax.sharding import PartitionSpec as P

D = 768
HEADS = 12
HEAD_DIM = 64
LANES = 128
TILE = 128
FF_BLOCK = 512
SQRT_HALF = math.sqrt(0.5)
INV_SQRT_2PI = 1.0 / math.sqrt(2.0 * math.pi)
VMEM_BYTES = 60000 * 1024


def dot(a, b, ca, cb):
    return lax.dot_general(a, b, (((ca,), (cb,)), ((), ())), preferred_element_type=jnp.float32)


def widths_for(length):
    return [w for w in (256, 384, 512, 768) if w < length] + [length]


def select_width(length, tile, low, high, run):
    first = low[tile]
    count = high[tile] - first
    previous = 0
    for width in widths_for(length):
        tiles = width // TILE

        @pl.when(jnp.logical_and(count > previous, count <= tiles))
        def _(width=width, tiles=tiles):
            start = jnp.minimum(first, length // TILE - tiles) * TILE
            run(width, pl.multiple_of(start, TILE))

        previous = tiles


def stack_heads(pair, lane_low):
    zero = jnp.zeros_like(pair)
    return jnp.concatenate([jnp.where(lane_low, pair, zero), jnp.where(lane_low, zero, pair)], axis=0)


def attend_kernel(low, high, mixed, label_col, label_row, attended, log_mass):
    length = mixed.shape[0]
    tile = pl.program_id(0)
    rows = pl.ds(pl.multiple_of(tile * TILE, TILE), TILE)
    lane = lax.broadcasted_iota(jnp.int32, (TILE, LANES), 1)
    lane_low = lane < HEAD_DIM

    def run(width, start):
        keys = pl.ds(start, width)
        allowed = label_col[rows, :] == label_row[:, keys]
        bias = jnp.where(allowed, 0.0, -1e30)
        bias = jnp.concatenate([bias, bias], axis=0)

        def pair_step(pair, masses):
            offset = pl.multiple_of(pair * LANES, LANES)
            query = mixed[rows, pl.ds(offset, LANES)] * jnp.bfloat16(0.125)
            key = mixed[keys, pl.ds(offset + D, LANES)]
            value = mixed[keys, pl.ds(offset + 2 * D, LANES)]
            scores = dot(stack_heads(query, lane_low), key, 1, 1) + bias
            peak = jnp.max(scores, axis=1, keepdims=True)
            expo = jnp.exp(scores - peak)
            total = jnp.sum(expo, axis=1, keepdims=True)
            both = dot(expo.astype(jnp.bfloat16), value, 1, 0) / total
            attended[:, pl.ds(offset, LANES)] = jnp.where(
                lane_low, both[:TILE], both[TILE:]
            ).astype(jnp.bfloat16)
            mass = peak + jnp.log(total)
            masses = jnp.where(lane == 2 * pair, mass[:TILE], masses)
            return jnp.where(lane == 2 * pair + 1, mass[TILE:], masses)

        log_mass[...] = lax.fori_loop(
            0, HEADS // 2, pair_step, jnp.zeros((TILE, LANES), jnp.float32)
        )

    select_width(length, tile, low, high, run)


def attend_back_kernel(
    low, high, mixed, label_col, label_row, log_mass, attended, grad_att, grad_mixed, key_acc, value_acc
):
    length = mixed.shape[0]
    tile = pl.program_id(0)
    rows = pl.ds(pl.multiple_of(tile * TILE, TILE), TILE)
    lane = lax.broadcasted_iota(jnp.int32, (TILE, LANES), 1)
    lane_low = lane < HEAD_DIM

    @pl.when(tile == 0)
    def _():
        key_acc[...] = jnp.zeros_like(key_acc)
        value_acc[...] = jnp.zeros_like(value_acc)

    def run(width, start):
        keys = pl.ds(start, width)
        allowed = label_col[rows, :] == label_row[:, keys]
        bias = jnp.where(allowed, 0.0, -1e30)
        bias = jnp.concatenate([bias, bias], axis=0)
        masses = log_mass[...]

        def pair_step(pair, carry):
            offset = pl.multiple_of(pair * LANES, LANES)
            lanes = pl.ds(offset, LANES)
            query = stack_heads(mixed[rows, lanes] * jnp.bfloat16(0.125), lane_low)
            key = mixed[keys, pl.ds(offset + D, LANES)]
            value = mixed[keys, pl.ds(offset + 2 * D, LANES)]
            grad = grad_att[:, lanes]
            product = grad.astype(jnp.float32) * attended[:, lanes].astype(jnp.float32)
            delta = jnp.concatenate(
                [
                    jnp.sum(jnp.where(lane_low, product, 0.0), axis=1, keepdims=True),
                    jnp.sum(jnp.where(lane_low, 0.0, product), axis=1, keepdims=True),
                ],
                axis=0,
            )
            mass = jnp.concatenate(
                [
                    jnp.sum(jnp.where(lane == 2 * pair, masses, 0.0), axis=1, keepdims=True),
                    jnp.sum(jnp.where(lane == 2 * pair + 1, masses, 0.0), axis=1, keepdims=True),
                ],
                axis=0,
            )
            grad_two = stack_heads(grad, lane_low)
            probs = jnp.exp(dot(query, key, 1, 1) + bias - mass)
            grad_probs = dot(grad_two, value, 1, 1)
            grad_scores = (probs * (grad_probs - delta)).astype(jnp.bfloat16)
            grad_query = dot(grad_scores, key, 1, 0) * 0.125
            grad_mixed[rows, lanes] = jnp.where(
                lane_low, grad_query[:TILE], grad_query[TILE:]
            ).astype(jnp.bfloat16)
            key_acc[keys, lanes] += dot(grad_scores, query, 0, 0)
            value_acc[keys, lanes] += dot(probs.astype(jnp.bfloat16), grad_two, 0, 0)
            return carry

        lax.fori_loop(0, HEADS // 2, pair_step, 0)

    select_width(length, tile, low, high, run)

    @pl.when(tile == pl.num_programs(0) - 1)
    def _():
        grad_mixed[:, D : 2 * D] = key_acc[...].astype(jnp.bfloat16)
        grad_mixed[:, 2 * D :] = value_acc[...].astype(jnp.bfloat16)


def attention_specs(length):
    whole = lambda i, *_: (0, 0)
    tiled = lambda i, *_: (i, 0)
    once = pl.Buffered(1)
    return (
        pl.BlockSpec((length, 3 * D), whole, pipeline_mode=once),
        pl.BlockSpec((length, 1), whole, pipeline_mode=once),
        pl.BlockSpec((1, length), whole, pipeline_mode=once),
        pl.BlockSpec((TILE, LANES), tiled),
        pl.BlockSpec((TILE, D), tiled),
    )


def attend(mixed, labels, low, high):
    length = mixed.shape[0]
    mixed_spec, col_spec, row_spec, mass_spec, rows_spec = attention_specs(length)
    return pl.pallas_call(
        attend_kernel,
        grid_spec=pltpu.PrefetchScalarGridSpec(
            num_scalar_prefetch=2,
            grid=(length // TILE,),
            in_specs=[mixed_spec, col_spec, row_spec],
            out_specs=[rows_spec, mass_spec],
        ),
        out_shape=[
            jax.ShapeDtypeStruct((length, D), jnp.bfloat16),
            jax.ShapeDtypeStruct((length, LANES), jnp.float32),
        ],
        compiler_params=pltpu.CompilerParams(vmem_limit_bytes=VMEM_BYTES),
        cost_estimate=pl.CostEstimate(
            flops=4 * length * 512 * D, bytes_accessed=length * 5 * D * 2, transcendentals=length * 512 * HEADS
        ),
        name="attend",
    )(low, high, mixed, labels[:, None], labels[None, :])


def attend_back(mixed, labels, low, high, log_mass, attended, grad_att):
    length = mixed.shape[0]
    mixed_spec, col_spec, row_spec, mass_spec, rows_spec = attention_specs(length)
    return pl.pallas_call(
        attend_back_kernel,
        grid_spec=pltpu.PrefetchScalarGridSpec(
            num_scalar_prefetch=2,
            grid=(length // TILE,),
            in_specs=[mixed_spec, col_spec, row_spec, mass_spec, rows_spec, rows_spec],
            out_specs=pl.BlockSpec((length, 3 * D), lambda i, *_: (0, 0)),
            scratch_shapes=[pltpu.VMEM((length, D), jnp.float32)] * 2,
        ),
        out_shape=jax.ShapeDtypeStruct((length, 3 * D), jnp.bfloat16),
        compiler_params=pltpu.CompilerParams(vmem_limit_bytes=VMEM_BYTES),
        cost_estimate=pl.CostEstimate(
            flops=10 * length * 512 * D, bytes_accessed=length * 9 * D * 2, transcendentals=length * 512 * HEADS
        ),
        name="attend_back",
    )(low, high, mixed, labels[:, None], labels[None, :], log_mass, attended, grad_att)


CHUNK = 256


def rise_kernel(normed, cotangent, up, up_bias, active, slope, grad_down):
    def row_step(index, carry):
        rows = pl.ds(pl.multiple_of(index * CHUNK, CHUNK), CHUNK)
        upward = dot(normed[rows, :], up[...], 1, 0) + up_bias[...]
        normal = 0.5 * (1.0 + lax.erf(upward * SQRT_HALF))
        density = jnp.exp(-0.5 * upward * upward) * INV_SQRT_2PI
        active[rows, :] = (upward * normal).astype(jnp.bfloat16)
        slope[rows, :] = normal + upward * density
        return carry

    lax.fori_loop(0, normed.shape[0] // CHUNK, row_step, 0)
    grad_down[...] = dot(active[...], cotangent[...], 0, 0).astype(jnp.bfloat16)


def fall_kernel(
    normed, cotangent, up, down, active, slope, middle, bias,
    out, back, grad_up, grad_bias, out_acc, grad_all,
):
    step = pl.program_id(0)
    last = step == pl.num_programs(0) - 1

    def row_step(index, total):
        rows = pl.ds(pl.multiple_of(index * CHUNK, CHUNK), CHUNK)
        grad_active = dot(cotangent[rows, :], down[...], 1, 1)
        grad_low = (grad_active * slope[rows, :]).astype(jnp.bfloat16)
        grad_all[rows, :] = grad_low
        forward = dot(active[rows, :], down[...], 1, 0)
        backward = dot(grad_low, up[...], 1, 1)

        @pl.when(step == 0)
        def _():
            out_acc[rows, :] = middle[rows, :] + bias[...] + forward
            back[rows, :] = backward

        @pl.when(step > 0)
        def _():
            out_acc[rows, :] += forward
            back[rows, :] += backward

        @pl.when(last)
        def _():
            out[rows, :] = out_acc[rows, :].astype(jnp.bfloat16)

        return total + jnp.sum(grad_low.astype(jnp.float32), axis=0, keepdims=True)

    grad_bias[...] = lax.fori_loop(
        0, normed.shape[0] // CHUNK, row_step, jnp.zeros((1, up.shape[1]), jnp.float32)
    )
    grad_up[...] = dot(normed[...], grad_all[...], 0, 0).astype(jnp.bfloat16)


def feed_specs(length, hidden):
    block = min(FF_BLOCK, hidden)
    whole = lambda i: (0, 0)
    return (
        hidden // block,
        block,
        pl.BlockSpec((length, D), whole, pipeline_mode=pl.Buffered(1)),
        pl.BlockSpec((D, block), lambda i: (0, i)),
        pl.BlockSpec((block, D), lambda i: (i, 0)),
        pl.BlockSpec((length, block), lambda i: (0, i)),
        pl.BlockSpec((1, block), lambda i: (0, i)),
        pl.BlockSpec((length, D), whole),
    )


def rise(normed, cotangent, up, up_bias):
    length, hidden = normed.shape[0], up.shape[1]
    steps, block, full, up_spec, down_spec, act_spec, bias_spec, _ = feed_specs(length, hidden)
    return pl.pallas_call(
        rise_kernel,
        grid=(steps,),
        in_specs=[full, full, up_spec, bias_spec],
        out_specs=[act_spec, act_spec, down_spec],
        out_shape=[
            jax.ShapeDtypeStruct((length, hidden), jnp.bfloat16),
            jax.ShapeDtypeStruct((length, hidden), jnp.float32),
            jax.ShapeDtypeStruct((hidden, D), jnp.bfloat16),
        ],
        compiler_params=pltpu.CompilerParams(vmem_limit_bytes=VMEM_BYTES),
        cost_estimate=pl.CostEstimate(
            flops=4 * length * hidden * D,
            bytes_accessed=length * hidden * 6 + hidden * D * 4 + length * D * 4,
            transcendentals=2 * length * hidden,
        ),
        name="rise",
    )(normed, cotangent, up, up_bias)


def fall(normed, cotangent, up, down, active, slope, middle, bias):
    length, hidden = normed.shape[0], up.shape[1]
    steps, block, full, up_spec, down_spec, act_spec, bias_spec, sum_spec = feed_specs(length, hidden)
    return pl.pallas_call(
        fall_kernel,
        grid=(steps,),
        in_specs=[
            full, full, up_spec, down_spec, act_spec, act_spec, full,
            pl.BlockSpec((1, D), lambda i: (0, 0)),
        ],
        out_specs=[sum_spec, sum_spec, up_spec, bias_spec],
        out_shape=[
            jax.ShapeDtypeStruct((length, D), jnp.bfloat16),
            jax.ShapeDtypeStruct((length, D), jnp.float32),
            jax.ShapeDtypeStruct((D, hidden), jnp.bfloat16),
            jax.ShapeDtypeStruct((1, hidden), jnp.float32),
        ],
        scratch_shapes=[
            pltpu.VMEM((length, D), jnp.float32),
            pltpu.VMEM((length, block), jnp.bfloat16),
        ],
        compiler_params=pltpu.CompilerParams(vmem_limit_bytes=VMEM_BYTES),
        cost_estimate=pl.CostEstimate(
            flops=8 * length * hidden * D,
            bytes_accessed=length * hidden * 6 + hidden * D * 6 + length * D * 14,
            transcendentals=0,
        ),
        name="fall",
    )(normed, cotangent, up, down, active, slope, middle, bias)


def position_rows(position_ids, frame_row):
    tubelet = position_ids // 196
    within = position_ids % 196
    halves = tubelet * 32 // frame_row
    channel = jnp.arange(D, dtype=jnp.int32)
    rate = jnp.exp(-(6.0 * (channel // 6).astype(jnp.float32) / D) * math.log(10000.0))
    entry = jnp.arange(48, dtype=jnp.int32)
    which = entry // 16
    level = (entry % 16).astype(jnp.float32) * jnp.where(which == 0, 0.5, 1.0)
    angle = level[:, None] * rate[None, :]
    values = jnp.where((channel // 3 % 2)[None, :] == 1, jnp.cos(angle), jnp.sin(angle))
    values = jnp.where(which[:, None] == (channel % 3)[None, :], values, 0.0)
    first = lax.reduce_precision(values, 8, 7)
    second = lax.reduce_precision(values - first, 8, 7)
    third = values - first - second
    table = jnp.concatenate([first, second, third], axis=0).astype(jnp.bfloat16)
    picks = [
        (index[:, None] + 16 * number) == entry[None, :]
        for number, index in enumerate((halves, within // 14, within % 14))
    ]
    hot = (picks[0] | picks[1] | picks[2]).astype(jnp.bfloat16)
    hot = jnp.concatenate([hot, hot, hot], axis=1)
    return jnp.dot(hot, table, preferred_element_type=jnp.float32)


def norm_parts(values):
    center = values - jnp.mean(values, axis=-1, keepdims=True)
    spread = jnp.mean(center * center, axis=-1, keepdims=True)
    rstd = lax.rsqrt(spread + 1e-06)
    return center * rstd, rstd


def norm_back(hat, rstd, gain, grad):
    e = grad * gain
    return rstd * (
        e - jnp.mean(e, axis=-1, keepdims=True) - hat * jnp.mean(e * hat, axis=-1, keepdims=True)
    )


def lane_rows(vectors):
    number = lax.broadcasted_iota(jnp.int32, (LANES, vectors[0].shape[0]), 0)
    result = jnp.zeros(number.shape, vectors[0].dtype)
    for k, vector in enumerate(vectors):
        result = jnp.where(number == k, vector[None, :], result)
    return result


def gather(values):
    return lax.all_gather(values, "wide", axis=0, tiled=True)


def scatter(values):
    return lax.psum_scatter(values, "wide", scatter_dimension=0, tiled=True)


def per_device(narrow, wide, *args):
    (
        tokens, frame_counts, segment_ids, positions, cotangent,
        input_weight, output_weight, up_weight, down_weight,
        pre_gain, pre_bias, query_bias, value_bias, output_bias,
        mid_gain, mid_bias, up_bias, down_bias,
    ) = args
    length = tokens.shape[0]
    rows = pre_gain.shape[0]

    def sum_copies(values):
        half = values.shape[0] // 2
        pieces = [values[:half], values[half:]]
        bits = [1 << k for k in range(narrow.bit_length() - 1)]
        outs = []
        for piece, order in zip(pieces, (bits, bits[::-1])):
            for bit in order:
                other = lax.ppermute(piece, "narrow", [(i, i ^ bit) for i in range(narrow)])
                piece = (piece.astype(jnp.float32) + other.astype(jnp.float32)).astype(jnp.bfloat16)
            outs.append(piece)
        return jnp.concatenate(outs, axis=0)

    quarters = up_bias.shape[0] // rows
    singles = [pre_gain, pre_bias, query_bias, value_bias, output_bias, mid_gain, mid_bias, down_bias]
    vectors = lane_rows(singles + list(up_bias.reshape(quarters, rows))).T
    packed = gather(jnp.concatenate([input_weight, output_weight, vectors], axis=1))
    full_input = packed[:, : 3 * D]
    full_output = packed[:, 3 * D : 4 * D]
    full_vectors = packed[:, 4 * D :].T.astype(jnp.float32)
    g_pre, b_pre, b_query, b_value, b_output, g_mid, b_mid, b_down = [full_vectors[k] for k in range(8)]
    full_up_bias = full_vectors[8 : 8 + quarters].reshape(quarters, wide, rows)
    full_up_bias = full_up_bias.transpose(1, 0, 2).reshape(1, -1)
    full_up = gather(up_weight)
    full_down = gather(down_weight)

    clip_index = jnp.arange(frame_counts.shape[1], dtype=jnp.int32)
    frame_row = jnp.sum(
        jnp.where(segment_ids[:, None] == clip_index[None, :], frame_counts, 0), axis=1
    )
    start = tokens.astype(jnp.float32) + position_rows(positions, frame_row)
    start = lax.optimization_barrier(start)
    hat, rstd = norm_parts(start)
    normed = (hat * g_pre + b_pre).astype(jnp.bfloat16)
    joint_bias = jnp.concatenate([b_query, jnp.zeros_like(b_query), b_value])
    mixed = (jnp.dot(normed, full_input, preferred_element_type=jnp.float32) + joint_bias).astype(
        jnp.bfloat16
    )
    tiles = segment_ids.reshape(length // TILE, TILE)
    low = jnp.sum((segment_ids[None, :] < tiles[:, :1]).astype(jnp.int32), axis=1) // TILE
    high = (
        jnp.sum((segment_ids[None, :] <= tiles[:, -1:]).astype(jnp.int32), axis=1) + TILE - 1
    ) // TILE
    attended, log_mass = attend(mixed, segment_ids, low, high)
    middle = (
        start + jnp.dot(attended, full_output, preferred_element_type=jnp.float32) + b_output
    )
    middle = lax.optimization_barrier(middle)
    hat_two, rstd_two = norm_parts(middle)
    normed_two = (hat_two * g_mid + b_mid).astype(jnp.bfloat16)

    active, slope, grad_down = rise(normed_two, cotangent, full_up, full_up_bias)
    down_share = sum_copies(scatter(grad_down))
    block_out, back_sum, grad_up, grad_bias = fall(
        normed_two, cotangent, full_up, full_down, active, slope, middle, b_down[None, :]
    )
    up_share = sum_copies(scatter(grad_up))
    grad_top = cotangent.astype(jnp.float32)
    grad_middle = grad_top + norm_back(hat_two, rstd_two, g_mid, back_sum)
    grad_middle = lax.optimization_barrier(grad_middle)
    branch = grad_middle.astype(jnp.bfloat16)
    grad_up_bias = grad_bias.reshape(wide, quarters, rows).transpose(1, 0, 2).reshape(quarters, D)
    first_rows = [
        jnp.sum(branch.astype(jnp.float32), axis=0),
        jnp.sum(back_sum * hat_two, axis=0),
        jnp.sum(back_sum, axis=0),
        jnp.sum(grad_top, axis=0),
    ] + list(grad_up_bias)
    grad_output = dot(attended, branch, 0, 0).astype(jnp.bfloat16)

    grad_att = dot(branch, full_output, 1, 1).astype(jnp.bfloat16)
    grad_mixed = attend_back(mixed, segment_ids, low, high, log_mass, attended, grad_att)
    grad_input = dot(normed, grad_mixed, 0, 0).astype(jnp.bfloat16)
    grad_normed = dot(grad_mixed, full_input, 1, 1)
    grad_normed = lax.optimization_barrier(grad_normed)
    mixed_sum = jnp.sum(grad_mixed.astype(jnp.float32), axis=0)
    last_rows = [
        jnp.sum(grad_normed * hat, axis=0),
        jnp.sum(grad_normed, axis=0),
        mixed_sum[:D],
        mixed_sum[2 * D :],
    ]
    grad_vectors = lane_rows(first_rows + last_rows).astype(jnp.bfloat16).T
    share = sum_copies(scatter(jnp.concatenate([grad_input, grad_output, grad_vectors], axis=1)))
    input_grad = (grad_middle + norm_back(hat, rstd, g_pre, grad_normed)).astype(jnp.bfloat16)

    f32 = lambda values: values.astype(jnp.float32)
    summed = f32(share[:, 4 * D :]).T
    last = 4 + quarters
    return (
        block_out,
        input_grad,
        f32(share[:, : 3 * D]),
        f32(share[:, 3 * D : 4 * D]),
        f32(up_share),
        f32(down_share),
        summed[last],
        summed[last + 1],
        summed[last + 2],
        summed[last + 3],
        summed[0],
        summed[1],
        summed[2],
        summed[4:last].reshape(-1),
        summed[3],
    )


def solution(mesh):
    both = ("narrow", "wide")
    in_specs = (
        (P(both, None), P(both, None), P(both), P(both), P(both, None))
        + (P("wide", None),) * 4
        + (P("wide"),) * 9
    )
    out_specs = (P(both, None),) * 2 + (P("wide", None),) * 4 + (P("wide"),) * 9
    return jax.shard_map(
        partial(per_device, mesh.shape["narrow"], mesh.shape["wide"]),
        mesh=mesh, in_specs=in_specs, out_specs=out_specs, check_vma=False,
    )
```
